32 devices in a mesh: row: 8 (over z, core), col: 4 (over y, x).
Axes of the slice: x: 2, y: 2, z: 4, core: 2. Of those that a mesh axis runs over, the one named last changes fastest.
Arguments:
- inputs: bfloat16 [2, 64, 8192], P(None, None, 'col'), may hold values from -6 to 6
- w_input: bfloat16 [2, 4, 8192, 8192], P(None, None, 'row', 'col'), may hold values from -0.0625 to 0.0625
- w_recur: bfloat16 [2, 4, 8192, 8192], P(None, None, 'row', 'col'), may hold values from -0.0625 to 0.0625
- gate_bias: float32 [2, 4, 8192], P(None, None, 'row'), may hold values from -1 to 2
- hidden_init: bfloat16 [2, 64, 8192], P(None, None, ('row', 'col')), may hold values from -3 to 3
- cell_init: float32 [2, 64, 8192], P(None, None, ('row', 'col')), may hold values from -6 to 6
Outputs:
- top_hidden: bfloat16 [2, 64, 8192], P(None, None, ('row', 'col'))
- final_hidden: bfloat16 [2, 64, 8192], P(None, None, ('row', 'col'))
- final_cell: float32 [2, 64, 8192], P(None, None, ('row', 'col'))
The draws below stay inside these ranges and needn't reach their ends.
All inputs are finite; a program needn't handle non-finite values.
Results may differ from the reference program's by a relative error of at most 0.009.
Values may be sent and summed in bfloat16 or wider, within the bound.
A program may use at most 128 MiB of HBM per device.

```python
import jax
import jax.numpy as jnp
from jax import lax

H = 8192
BATCH = 64
STEPS = 2
LAYERS = 2
UNIT = 256
N_ROW = 8
N_COL = 4


def with_spikes(drawn, rng, source, target, parts, factor):
    owner, partner = [(jnp.arange(drawn.shape[dim]) // (drawn.shape[dim] // parts)).reshape([-1 if axis == dim else 1 for axis in range(drawn.ndim)]) for dim in (source, target)]
    chosen = jax.random.permutation(rng, parts)[partner]
    strong = (owner == chosen) | (owner == (partner + parts // 2) % parts)
    return jnp.where(strong, factor * drawn, drawn)


def block_levels(own_key, extent, pieces, least, high):
    loudness, own = 1.0, jax.random.fold_in(own_key, 6)
    for axis_at, blocks in pieces:
        steps = jnp.exp(jax.random.uniform(jax.random.fold_in(own, axis_at), (blocks,), jnp.float32, least / len(pieces), high / len(pieces)))
        loudness = loudness * jnp.repeat(steps, extent[axis_at] // blocks).reshape([-1 if axis == axis_at else 1 for axis in range(len(extent))])
    return loudness


def normal_values(stream_key, extent, spread, reach, pieces=(), kind=jnp.bfloat16):
    loudness = block_levels(stream_key, extent, pieces, -0.22, 0.18) if pieces else 1.0
    drawn = jax.random.normal(stream_key, extent, jnp.float32) * spread * loudness
    return jnp.minimum(jnp.maximum(drawn, -reach), reach).astype(kind)


def gaussian_with(rng, extent, spread, bound, cuts, heavy, held_as=jnp.bfloat16):
    drawn = spread * jax.random.normal(rng, extent, jnp.float32)
    if cuts:
        drawn = drawn * block_levels(rng, extent, cuts, -0.22, 0.18)
    return jnp.clip(with_spikes(drawn, jax.random.fold_in(rng, 3), *heavy), -bound, bound).astype(held_as)


def setup_inputs(seed: int = 0) -> dict:
    streams_of = jax.random.split(jax.random.key(seed), 7)
    return {
        "inputs": normal_values(streams_of[0], (STEPS, BATCH, H), 1.0, 6.0, ((2, 4),)),
        "w_input": gaussian_with(streams_of[1], (LAYERS, 4, H, H), (2 * H) ** -0.5, 0.0625, ((2, 8), (3, 4)), (3, 2, 8, 2.0)),
        "w_recur": gaussian_with(streams_of[2], (LAYERS, 4, H, H), (2 * H) ** -0.5, 0.0625, ((2, 8), (3, 4)), (3, 2, 8, 2.0)),
        "gate_bias": jnp.clip(-1.0 + 3.0 * jax.random.uniform(streams_of[3], (LAYERS, 4, H), jnp.float32) ** block_levels(streams_of[3], (LAYERS, 4, H), ((2, 8),), -0.2, 0.2), -1.0, 2.0),
        "hidden_init": normal_values(streams_of[4], (LAYERS, BATCH, H), 0.5, 3.0, ((2, 32),)),
        "cell_init": normal_values(streams_of[5], (LAYERS, BATCH, H), 1.0, 6.0, ((2, 32),), jnp.float32),
    }


def to_positions(hidden):
    count = hidden.shape[0]
    return hidden.reshape(count, N_ROW, N_COL, UNIT).transpose(0, 2, 1, 3).reshape(count, H)


def project(vectors, weight):
    count = vectors.shape[0]
    result = lax.dot_general(vectors, weight.reshape(4 * H, H), (((1,), (1,)), ((), ())), preferred_element_type=jnp.float32)
    return result.reshape(count, 4, H)


def lstm_cell(gate_total, cell_state):
    input_gate = jax.nn.sigmoid(gate_total[:, 0])
    forget_gate = jax.nn.sigmoid(gate_total[:, 1])
    candidate = jnp.tanh(gate_total[:, 2])
    output_gate = jax.nn.sigmoid(gate_total[:, 3])
    cell_state = forget_gate * cell_state + input_gate * candidate
    return cell_state, (output_gate * jnp.tanh(cell_state)).astype(jnp.bfloat16)


def reference(inputs, w_input, w_recur, gate_bias, hidden_init, cell_init):
    hiddens = [hidden_init[layer] for layer in range(LAYERS)]
    cells = [cell_init[layer] for layer in range(LAYERS)]
    top_rows = []
    for step in range(STEPS):
        lower_input = inputs[step]
        for layer in range(LAYERS):
            gate_total = project(lower_input, w_input[layer]) + project(to_positions(hiddens[layer]), w_recur[layer]) + gate_bias[layer][None]
            cells[layer], hiddens[layer] = lstm_cell(gate_total, cells[layer])
            lower_input = to_positions(hiddens[layer])
        top_rows.append(hiddens[-1])
    return jnp.stack(top_rows), jnp.stack(hiddens), jnp.stack(cells)
```

```python
import functools

import jax
import jax.numpy as jnp
from jax import lax
from jax.experimental import pallas as pl
from jax.experimental.pallas import tpu as pltpu
from jax.sharding import PartitionSpec as P

MESH = pl.DeviceIdType.MESH
GATES = 4
LOCAL_VMEM = 67_043_328


def lstm_cell(gate_total, cell_state):
    input_gate = jax.nn.sigmoid(gate_total[:, 0])
    forget_gate = jax.nn.sigmoid(gate_total[:, 1])
    candidate = jnp.tanh(gate_total[:, 2])
    output_gate = jax.nn.sigmoid(gate_total[:, 3])
    cell_state = forget_gate * cell_state + input_gate * candidate
    return (cell_state, (output_gate * jnp.tanh(cell_state)).astype(jnp.bfloat16))


def general_body(inputs, w_input, w_recur, gate_bias, hidden_init, cell_init):
    col_place = lax.axis_index("col")
    unit_width = hidden_init.shape[2]
    layers = w_input.shape[0]
    block_rows = w_input.shape[2]

    def project(vectors, weight):
        result = lax.dot_general(
            vectors,
            weight.reshape(-1, weight.shape[-1]),
            (((1,), (1,)), ((), ())),
            preferred_element_type=jnp.float32,
        )
        return result.reshape(vectors.shape[:-1] + (GATES, block_rows))

    def to_columns(owned):
        return lax.all_gather(owned, "row", axis=1, tiled=True)

    def gate_sums(partial_value, layer):
        bias_part = lax.dynamic_slice_in_dim(
            gate_bias[layer], col_place * unit_width, unit_width, 1
        )
        return (
            lax.psum_scatter(
                partial_value.astype(jnp.bfloat16), "col", scatter_dimension=2, tiled=True
            ).astype(jnp.float32)
            + bias_part[None]
        )

    start = tuple(
        (hidden_init[layer], to_columns(hidden_init[layer]), cell_init[layer])
        for layer in range(layers)
    )

    def advance_time(carried, step_item):
        lower, following = step_item, []
        for layer in range(layers):
            _, columns, cell_state = carried[layer]
            partial_value = project(lower, w_input[layer]) + project(columns, w_recur[layer])
            cell_state, owned = lstm_cell(gate_sums(partial_value, layer), cell_state)
            lower = to_columns(owned)
            following.append((owned, lower, cell_state))
        return tuple(following), following[-1][0]

    carried, top_hidden = lax.scan(advance_time, start, inputs)
    return (
        top_hidden,
        jnp.stack([item[0] for item in carried]),
        jnp.stack([item[2] for item in carried]),
    )


def xor(value, mask, size):
    total, bit = 0, 1
    while bit < size:
        total = total + bit * ((value // bit + mask // bit) % 2)
        bit *= 2
    return total


def window_kernel(
    n_row, n_col,
    inputs, w_input, w_recur, gate_bias, hidden_init, cell_init,
    top_hidden, final_hidden, final_cell,
    first, second, third, sums, sent, arrived, columns,
    first_sem, first_again_sem, second_sem, third_sem,
    part_send, part_recv, block_send, block_recv,
):
    row, col = lax.axis_index("row"), lax.axis_index("col")
    unit = hidden_init.shape[2]
    batch = hidden_init.shape[1]
    chips = n_row // 2
    last = n_col - 1
    sibling = row + 1 - 2 * (row % 2)

    def owner_of(i):
        return xor(col, last - i, n_col)

    def load(weight, layer, buffer, sems, i, g):
        start = pl.multiple_of(owner_of(i) * unit, unit)
        k = i * GATES + g
        return pltpu.make_async_copy(
            weight.at[layer, g, pl.ds(start, unit), :], buffer.at[k], sems.at[k]
        )

    def far(k):
        return (row + 2 * k) % n_row

    def near(k):
        return (row + n_row - 2 * k) % n_row

    def send_block(which, source, owner, target, slot):
        return pltpu.make_async_remote_copy(
            src_ref=source,
            dst_ref=columns.at[which, owner],
            send_sem=block_send.at[which, slot],
            recv_sem=block_recv.at[which, slot],
            device_id=(target, col),
            device_id_type=MESH,
        )

    def gather_start(which, source):
        for k in range(1, chips):
            send_block(which, source, row, far(k), k).start()
        send_block(which, source, row, sibling, 0).start()

    def gather_forward(which):
        for k in range(1, chips):
            owner = near(k)
            send_block(which, columns.at[which, owner], owner, far(k), k).wait_recv()
            send_block(
                which, columns.at[which, owner], owner, sibling, chips - 1 + k
            ).start()

    def gather_wait(which):
        block = columns.at[which, sibling]
        send_block(which, block, sibling, sibling, 0).wait_recv()
        for k in range(1, chips):
            block = columns.at[which, (sibling + n_row - 2 * k) % n_row]
            send_block(which, block, row, sibling, chips - 1 + k).wait_recv()

    def gather_end(which):
        for slot in range(2 * chips - 1):
            send_block(which, columns.at[which, row], row, sibling, slot).wait_send()

    def vectors(which):
        return jnp.concatenate([columns[which, r] for r in range(n_row)], axis=1)

    def product(left, buffer, k):
        return lax.dot_general(
            left, buffer[k], (((1,), (1,)), ((), ())), preferred_element_type=jnp.float32
        )

    def send_part(which, i):
        return pltpu.make_async_remote_copy(
            src_ref=sent.at[which, i],
            dst_ref=arrived.at[which, i],
            send_sem=part_send.at[which, i],
            recv_sem=part_recv.at[which, i],
            device_id=(row, owner_of(i)),
            device_id_type=MESH,
        )

    def finish(which, held, buffer, i, before=None):
        left = vectors(held)
        totals = []
        for g in range(GATES):
            if before is not None:
                before(i, g)
            k = i * GATES + g
            totals.append(sums[which, k] + product(left, buffer, k))

        @pl.when(i < last)
        def _():
            for g in range(GATES):
                sent[which, i, g] = totals[g].astype(jnp.bfloat16)
            send_part(which, i).start()

        @pl.when(i == last)
        def _():
            for g in range(GATES):
                sums[which, last * GATES + g] = totals[g]

    def cell_step(which, layer, old_cell):
        for i in range(last):
            send_part(which, i).wait_recv()
        totals = []
        for g in range(GATES):
            total = sums[which, last * GATES + g]
            for i in range(last):
                total = total + arrived[which, i, g].astype(jnp.float32)
            bias = gate_bias[layer, pl.ds(g, 1), pl.ds(pl.multiple_of(col * unit, unit), unit)]
            totals.append(total + bias)
        cell = jax.nn.sigmoid(totals[1]) * old_cell + jax.nn.sigmoid(totals[0]) * jnp.tanh(totals[2])
        hidden = (jax.nn.sigmoid(totals[3]) * jnp.tanh(cell)).astype(jnp.bfloat16)
        return cell, hidden

    def loop(begin, end, step):
        def run(i, carried):
            step(i)
            return carried
        lax.fori_loop(begin, end, run, 0)

    for i in range(n_col):
        for g in range(GATES):
            load(w_input, 0, first, first_sem, i, g).start()
    for i in range(n_col):
        for g in range(GATES):
            load(w_recur, 0, second, second_sem, i, g).start()

    barrier = pltpu.get_barrier_semaphore()
    targets = [(sibling, col)]
    targets += [(far(k), col) for k in range(1, chips)]
    targets += [(row, owner_of(i)) for i in range(last)]
    for target in targets:
        pl.semaphore_signal(barrier, inc=1, device_id=target, device_id_type=MESH)
    pl.semaphore_wait(barrier, len(targets))

    for layer in range(2):
        gather_start(layer, hidden_init.at[layer])
        columns[layer, row] = hidden_init[layer]

    def input_products(i):
        left = inputs[...].reshape(2 * batch, inputs.shape[2])
        for g in range(GATES):
            k = i * GATES + g
            load(w_input, 0, first, first_sem, i, g).wait()
            both = product(left, first, k)
            sums[0, k] = both[:batch]
            sums[1, k] = both[batch:]

    half = n_col // 2
    loop(0, half, input_products)
    gather_forward(0)
    loop(half, n_col, input_products)
    gather_forward(1)
    gather_wait(0)

    def layer0_step0(i):
        def before(i, g):
            load(w_recur, 0, second, second_sem, i, g).wait()
            load(w_recur, 1, first, first_again_sem, i, g).start()

        finish(0, 0, second, i, before)

    loop(0, n_col, layer0_step0)
    for i in range(n_col):
        for g in range(GATES):
            load(w_input, 1, third, third_sem, i, g).start()
    gather_wait(1)

    def early_recurrent(i):
        left = vectors(1)
        for g in range(GATES):
            k = i * GATES + g
            load(w_recur, 1, first, first_again_sem, i, g).wait()
            sums[2, k] = product(left, first, k)

    loop(0, half, early_recurrent)
    cell, hidden = cell_step(0, 0, cell_init[0])
    columns[2, row] = hidden
    gather_start(2, columns.at[2, row])
    final_cell[0] = cell
    loop(half, n_col, early_recurrent)
    gather_forward(2)
    gather_wait(2)

    loop(0, n_col, lambda i: finish(1, 2, second, i))

    def layer1_step0(i):
        finish(2, 2, third, i, lambda i, g: load(w_input, 1, third, third_sem, i, g).wait())

    loop(0, half, layer1_step0)
    cell, hidden = cell_step(1, 0, final_cell[0])
    columns[3, row] = hidden
    gather_start(3, columns.at[3, row])
    final_cell[0] = cell
    final_hidden[0] = hidden
    loop(half, n_col, layer1_step0)
    gather_forward(3)
    gather_wait(3)

    def late_input(i):
        left = vectors(3)
        for g in range(GATES):
            k = i * GATES + g
            sums[3, k] = product(left, third, k)

    loop(0, half, late_input)
    cell, hidden = cell_step(2, 1, cell_init[1])
    columns[4, row] = hidden
    gather_start(4, columns.at[4, row])
    final_cell[1] = cell
    top_hidden[0] = hidden
    loop(half, n_col, late_input)
    gather_forward(4)
    gather_wait(4)
    loop(0, n_col, lambda i: finish(3, 4, first, i))
    cell, hidden = cell_step(3, 1, final_cell[1])
    final_cell[1] = cell
    top_hidden[1] = hidden
    final_hidden[1] = hidden

    for which in range(5):
        gather_end(which)
    for which in range(4):
        for i in range(last):
            send_part(which, i).wait_send()


def window_body(n_row, n_col, inputs, w_input, w_recur, gate_bias, hidden_init, cell_init):
    batch, unit = hidden_init.shape[1:]
    depth = w_input.shape[3]
    chunks = n_col * GATES
    chips = n_row // 2
    vmem = pl.BlockSpec(memory_space=pltpu.VMEM)
    hbm = pl.BlockSpec(memory_space=pl.ANY)
    return pl.pallas_call(
        functools.partial(window_kernel, n_row, n_col),
        out_shape=(
            jax.ShapeDtypeStruct((2, batch, unit), jnp.bfloat16),
            jax.ShapeDtypeStruct((2, batch, unit), jnp.bfloat16),
            jax.ShapeDtypeStruct((2, batch, unit), jnp.float32),
        ),
        in_specs=[vmem, hbm, hbm, vmem, vmem, vmem],
        out_specs=(vmem, vmem, vmem),
        scratch_shapes=[
            pltpu.VMEM((chunks, unit, depth), jnp.bfloat16),
            pltpu.VMEM((chunks, unit, depth), jnp.bfloat16),
            pltpu.VMEM((chunks, unit, depth), jnp.bfloat16),
            pltpu.VMEM((4, chunks, batch, unit), jnp.float32),
            pltpu.VMEM((4, n_col - 1, GATES, batch, unit), jnp.bfloat16),
            pltpu.VMEM((4, n_col - 1, GATES, batch, unit), jnp.bfloat16),
            pltpu.VMEM((5, n_row, batch, unit), jnp.bfloat16),
            pltpu.SemaphoreType.DMA((chunks,)),
            pltpu.SemaphoreType.DMA((chunks,)),
            pltpu.SemaphoreType.DMA((chunks,)),
            pltpu.SemaphoreType.DMA((chunks,)),
            pltpu.SemaphoreType.DMA((4, n_col - 1)),
            pltpu.SemaphoreType.DMA((4, n_col - 1)),
            pltpu.SemaphoreType.DMA((5, 2 * chips - 1)),
            pltpu.SemaphoreType.DMA((5, 2 * chips - 1)),
        ],
        compiler_params=pltpu.CompilerParams(
            collective_id=0, has_side_effects=True, vmem_limit_bytes=LOCAL_VMEM
        ),
    )(inputs, w_input, w_recur, gate_bias, hidden_init, cell_init)


def solution(mesh):
    n_row, n_col = mesh.shape["row"], mesh.shape["col"]

    def body(inputs, w_input, w_recur, gate_bias, hidden_init, cell_init):
        unit = hidden_init.shape[2]
        held = 3 * w_input.size // w_input.shape[0] * 2
        fits = (
            inputs.shape[0] == 2
            and w_input.shape[0] == 2
            and unit % 128 == 0
            and n_row % 2 == 0
            and n_row >= 4
            and n_col >= 2
            and n_col & (n_col - 1) == 0
            and held + held // 4 < LOCAL_VMEM
        )
        args = (inputs, w_input, w_recur, gate_bias, hidden_init, cell_init)
        return window_body(n_row, n_col, *args) if fits else general_body(*args)

    in_specs = (
        P(None, None, "col"),
        P(None, None, "row", "col"),
        P(None, None, "row", "col"),
        P(None, None, "row"),
        P(None, None, ("row", "col")),
        P(None, None, ("row", "col")),
    )
    out_specs = (
        P(None, None, ("row", "col")),
        P(None, None, ("row", "col")),
        P(None, None, ("row", "col")),
    )
    return jax.shard_map(body, mesh=mesh, in_specs=in_specs, out_specs=out_specs, check_vma=False)
```

```python
import functools

import jax
import jax.numpy as jnp
from jax import lax
from jax.experimental import pallas as pl
from jax.experimental.pallas import tpu as pltpu
from jax.sharding import PartitionSpec as P

MESH = pl.DeviceIdType.MESH
GATES = 4
LOCAL_VMEM = 67_043_328


def lstm_cell(gate_total, cell_state):
    input_gate = jax.nn.sigmoid(gate_total[:, 0])
    forget_gate = jax.nn.sigmoid(gate_total[:, 1])
    candidate = jnp.tanh(gate_total[:, 2])
    output_gate = jax.nn.sigmoid(gate_total[:, 3])
    cell_state = forget_gate * cell_state + input_gate * candidate
    return (cell_state, (output_gate * jnp.tanh(cell_state)).astype(jnp.bfloat16))


def general_body(inputs, w_input, w_recur, gate_bias, hidden_init, cell_init):
    col_place = lax.axis_index("col")
    unit_width = hidden_init.shape[2]
    layers = w_input.shape[0]
    block_rows = w_input.shape[2]

    def project(vectors, weight):
        result = lax.dot_general(
            vectors,
            weight.reshape(-1, weight.shape[-1]),
            (((1,), (1,)), ((), ())),
            preferred_element_type=jnp.float32,
        )
        return result.reshape(vectors.shape[:-1] + (GATES, block_rows))

    def to_columns(owned):
        return lax.all_gather(owned, "row", axis=1, tiled=True)

    def gate_sums(partial_value, layer):
        bias_part = lax.dynamic_slice_in_dim(
            gate_bias[layer], col_place * unit_width, unit_width, 1
        )
        return (
            lax.psum_scatter(
                partial_value.astype(jnp.bfloat16), "col", scatter_dimension=2, tiled=True
            ).astype(jnp.float32)
            + bias_part[None]
        )

    start = tuple(
        (hidden_init[layer], to_columns(hidden_init[layer]), cell_init[layer])
        for layer in range(layers)
    )

    def advance_time(carried, step_item):
        lower, following = step_item, []
        for layer in range(layers):
            _, columns, cell_state = carried[layer]
            partial_value = project(lower, w_input[layer]) + project(columns, w_recur[layer])
            cell_state, owned = lstm_cell(gate_sums(partial_value, layer), cell_state)
            lower = to_columns(owned)
            following.append((owned, lower, cell_state))
        return tuple(following), following[-1][0]

    carried, top_hidden = lax.scan(advance_time, start, inputs)
    return (
        top_hidden,
        jnp.stack([item[0] for item in carried]),
        jnp.stack([item[2] for item in carried]),
    )


def xor(value, mask, size):
    total, bit = 0, 1
    while bit < size:
        total = total + bit * ((value // bit + mask // bit) % 2)
        bit *= 2
    return total


def window_kernel(
    n_row, n_col,
    inputs_in, w_input, w_recur, gate_bias_in, hidden_init_in, cell_init_in,
    hiddens, cells,
    inputs, gate_bias, hidden_init, cell_init,
    first, second, third, sums, sent, arrived, columns, small_sem,
    first_sem, first_again_sem, second_sem, third_sem,
    part_send, part_recv, block_send, block_recv,
):
    row, col = lax.axis_index("row"), lax.axis_index("col")
    unit = hidden_init.shape[2]
    batch = hidden_init.shape[1]
    chips = n_row // 2
    last = n_col - 1
    sibling = row + 1 - 2 * (row % 2)

    def owner_of(i):
        return xor(col, last - i, n_col)

    def load(weight, layer, buffer, sems, i, g):
        start = pl.multiple_of(owner_of(i) * unit, unit)
        k = i * GATES + g
        return pltpu.make_async_copy(
            weight.at[layer, g, pl.ds(start, unit), :], buffer.at[k], sems.at[k]
        )

    def far(k):
        return (row + 2 * k) % n_row

    def near(k):
        return (row + n_row - 2 * k) % n_row

    def send_block(which, source, owner, target, slot):
        return pltpu.make_async_remote_copy(
            src_ref=source,
            dst_ref=columns.at[which, owner],
            send_sem=block_send.at[which, slot],
            recv_sem=block_recv.at[which, slot],
            device_id=(target, col),
            device_id_type=MESH,
        )

    def gather_start(which, source):
        for k in range(1, chips):
            send_block(which, source, row, far(k), k).start()
        send_block(which, source, row, sibling, 0).start()

    def gather_forward(which):
        for k in range(1, chips):
            owner = near(k)
            send_block(which, columns.at[which, owner], owner, far(k), k).wait_recv()
            send_block(
                which, columns.at[which, owner], owner, sibling, chips - 1 + k
            ).start()

    def gather_wait(which):
        block = columns.at[which, sibling]
        send_block(which, block, sibling, sibling, 0).wait_recv()
        for k in range(1, chips):
            block = columns.at[which, (sibling + n_row - 2 * k) % n_row]
            send_block(which, block, row, sibling, chips - 1 + k).wait_recv()

    def gather_end(which):
        for slot in range(2 * chips - 1):
            send_block(which, columns.at[which, row], row, sibling, slot).wait_send()

    def vectors(which):
        return jnp.concatenate([columns[which, r] for r in range(n_row)], axis=1)

    def product(left, buffer, k):
        return lax.dot_general(
            buffer[k], left, (((1,), (1,)), ((), ())), preferred_element_type=jnp.float32
        ).T

    def send_part(which, i):
        return pltpu.make_async_remote_copy(
            src_ref=sent.at[which, i],
            dst_ref=arrived.at[which, i],
            send_sem=part_send.at[which, i],
            recv_sem=part_recv.at[which, i],
            device_id=(row, owner_of(i)),
            device_id_type=MESH,
        )

    def finish(which, held, buffer, i):
        left = vectors(held)
        totals = []
        for g in range(GATES):
            k = i * GATES + g
            totals.append(sums[which, k] + product(left, buffer, k))

        @pl.when(i < last)
        def _():
            for g in range(GATES):
                sent[which, i, g] = totals[g].astype(jnp.bfloat16)
            send_part(which, i).start()

        @pl.when(i == last)
        def _():
            for g in range(GATES):
                sums[which, last * GATES + g] = totals[g]

    def cell_step(which, layer, old_cell):
        for i in range(last):
            send_part(which, i).wait_recv()
        totals = []
        for g in range(GATES):
            total = sums[which, last * GATES + g]
            for i in range(last):
                total = total + arrived[which, i, g].astype(jnp.float32)
            bias = gate_bias[layer, pl.ds(g, 1), pl.ds(pl.multiple_of(col * unit, unit), unit)]
            totals.append(total + bias)
        cell = jax.nn.sigmoid(totals[1]) * old_cell + jax.nn.sigmoid(totals[0]) * jnp.tanh(totals[2])
        hidden = (jax.nn.sigmoid(totals[3]) * jnp.tanh(cell)).astype(jnp.bfloat16)
        return cell, hidden

    def loop(begin, end, step):
        def run(i, carried):
            step(i)
            return carried
        lax.fori_loop(begin, end, run, 0)

    small = [
        pltpu.make_async_copy(source, target, small_sem.at[k])
        for k, (source, target) in enumerate((
            (hidden_init_in, hidden_init),
            (inputs_in, inputs),
            (gate_bias_in, gate_bias),
            (cell_init_in, cell_init),
        ))
    ]
    for copy in small:
        copy.start()

    streams = (
        (w_input, 0, first, first_sem),
        (w_recur, 0, second, second_sem),
        (w_recur, 1, first, first_again_sem),
        (w_input, 1, third, third_sem),
    )
    ahead = min(2, n_col)

    def load_start(which, i):
        for g in range(GATES):
            load(*streams[which], i, g).start()

    def load_wait(which, i):
        for g in range(GATES):
            load(*streams[which], i, g).wait()

    def next_loads(which, i):
        @pl.when(i + ahead < n_col)
        def _():
            load_start(which, i + ahead)

        if which + 1 < len(streams):
            @pl.when(i + ahead >= n_col)
            def _():
                load_start(which + 1, i + ahead - n_col)

    for i in range(ahead):
        load_start(0, i)

    barrier = pltpu.get_barrier_semaphore()
    targets = [(sibling, col)]
    targets += [(far(k), col) for k in range(1, chips)]
    targets += [(row, owner_of(i)) for i in range(last)]
    for target in targets:
        pl.semaphore_signal(barrier, inc=1, device_id=target, device_id_type=MESH)
    pl.semaphore_wait(barrier, len(targets))

    small[0].wait()
    for layer in range(2):
        gather_start(layer, hidden_init.at[layer])
        columns[layer, row] = hidden_init[layer]

    for copy in small[1:]:
        copy.wait()

    def input_products(i):
        load_wait(0, i)
        next_loads(0, i)
        left = inputs[...].reshape(2 * batch, inputs.shape[2])
        for g in range(GATES):
            k = i * GATES + g
            both = product(left, first, k)
            sums[0, k] = both[:batch]
            sums[1, k] = both[batch:]

    half = n_col // 2
    loop(0, half, input_products)
    gather_forward(0)
    loop(half, n_col, input_products)
    gather_forward(1)
    gather_wait(0)

    def layer0_step0(i):
        load_wait(1, i)
        next_loads(1, i)
        finish(0, 0, second, i)

    loop(0, n_col, layer0_step0)
    gather_wait(1)

    def early_recurrent(i):
        load_wait(2, i)
        next_loads(2, i)
        left = vectors(1)
        for g in range(GATES):
            k = i * GATES + g
            sums[2, k] = product(left, first, k)

    loop(0, half, early_recurrent)
    cell, hidden = cell_step(0, 0, cell_init[0])
    columns[2, row] = hidden
    gather_start(2, columns.at[2, row])
    cells[0] = cell
    loop(half, n_col, early_recurrent)
    for i in range(ahead, n_col):
        load_start(3, i)
    gather_forward(2)
    gather_wait(2)

    loop(0, n_col, lambda i: finish(1, 2, second, i))

    def layer1_step0(i):
        load_wait(3, i)
        finish(2, 2, third, i)

    loop(0, half, layer1_step0)
    cell, hidden = cell_step(1, 0, cells[0])
    columns[3, row] = hidden
    gather_start(3, columns.at[3, row])
    cells[0] = cell
    hiddens[2] = hidden
    loop(half, n_col, layer1_step0)
    gather_forward(3)
    gather_wait(3)

    def late_input(i):
        left = vectors(3)
        for g in range(GATES):
            k = i * GATES + g
            sums[3, k] = product(left, third, k)

    loop(0, half, late_input)
    cell, hidden = cell_step(2, 1, cell_init[1])
    columns[4, row] = hidden
    gather_start(4, columns.at[4, row])
    cells[1] = cell
    hiddens[0] = hidden
    loop(half, n_col, late_input)
    gather_forward(4)
    gather_wait(4)
    loop(0, n_col, lambda i: finish(3, 4, first, i))
    cell, hidden = cell_step(3, 1, cells[1])
    cells[1] = cell
    hiddens[1] = hidden

    for which in range(5):
        gather_end(which)
    for which in range(4):
        for i in range(last):
            send_part(which, i).wait_send()


def output_kernel(hiddens, cells, top_hidden, final_hidden, final_cell):
    top_hidden[...] = hiddens[:2]
    final_hidden[0] = hiddens[2]
    final_hidden[1] = hiddens[1]
    final_cell[...] = cells[...]


def window_body(n_row, n_col, inputs, w_input, w_recur, gate_bias, hidden_init, cell_init):
    batch, unit = hidden_init.shape[1:]
    depth = w_input.shape[3]
    chunks = n_col * GATES
    chips = n_row // 2
    vmem = pl.BlockSpec(memory_space=pltpu.VMEM)
    hbm = pl.BlockSpec(memory_space=pl.ANY)
    hiddens, cells = pl.pallas_call(
        functools.partial(window_kernel, n_row, n_col),
        out_shape=(
            jax.ShapeDtypeStruct((3, batch, unit), jnp.bfloat16),
            jax.ShapeDtypeStruct((2, batch, unit), jnp.float32),
        ),
        in_specs=[hbm] * 6,
        out_specs=(vmem, vmem),
        scratch_shapes=[
            pltpu.VMEM(inputs.shape, inputs.dtype),
            pltpu.VMEM(gate_bias.shape, gate_bias.dtype),
            pltpu.VMEM(hidden_init.shape, hidden_init.dtype),
            pltpu.VMEM(cell_init.shape, cell_init.dtype),
            pltpu.VMEM((chunks, unit, depth), jnp.bfloat16),
            pltpu.VMEM((chunks, unit, depth), jnp.bfloat16),
            pltpu.VMEM((chunks, unit, depth), jnp.bfloat16),
            pltpu.VMEM((4, chunks, batch, unit), jnp.float32),
            pltpu.VMEM((4, n_col - 1, GATES, batch, unit), jnp.bfloat16),
            pltpu.VMEM((4, n_col - 1, GATES, batch, unit), jnp.bfloat16),
            pltpu.VMEM((5, n_row, batch, unit), jnp.bfloat16),
            pltpu.SemaphoreType.DMA((4,)),
            pltpu.SemaphoreType.DMA((chunks,)),
            pltpu.SemaphoreType.DMA((chunks,)),
            pltpu.SemaphoreType.DMA((chunks,)),
            pltpu.SemaphoreType.DMA((chunks,)),
            pltpu.SemaphoreType.DMA((4, n_col - 1)),
            pltpu.SemaphoreType.DMA((4, n_col - 1)),
            pltpu.SemaphoreType.DMA((5, 2 * chips - 1)),
            pltpu.SemaphoreType.DMA((5, 2 * chips - 1)),
        ],
        compiler_params=pltpu.CompilerParams(
            collective_id=0, has_side_effects=True, vmem_limit_bytes=LOCAL_VMEM
        ),
    )(inputs, w_input, w_recur, gate_bias, hidden_init, cell_init)
    return pl.pallas_call(
        output_kernel,
        out_shape=(
            jax.ShapeDtypeStruct((2, batch, unit), jnp.bfloat16),
            jax.ShapeDtypeStruct((2, batch, unit), jnp.bfloat16),
            jax.ShapeDtypeStruct((2, batch, unit), jnp.float32),
        ),
        in_specs=[vmem, vmem],
        out_specs=(vmem, vmem, vmem),
    )(hiddens, cells)


def solution(mesh):
    n_row, n_col = mesh.shape["row"], mesh.shape["col"]

    def body(inputs, w_input, w_recur, gate_bias, hidden_init, cell_init):
        unit = hidden_init.shape[2]
        held = 3 * w_input.size // w_input.shape[0] * 2
        fits = (
            inputs.shape[0] == 2
            and w_input.shape[0] == 2
            and unit % 128 == 0
            and n_row % 2 == 0
            and n_row >= 4
            and n_col >= 2
            and n_col & (n_col - 1) == 0
            and held + held // 4 < LOCAL_VMEM
        )
        args = (inputs, w_input, w_recur, gate_bias, hidden_init, cell_init)
        return window_body(n_row, n_col, *args) if fits else general_body(*args)

    in_specs = (
        P(None, None, "col"),
        P(None, None, "row", "col"),
        P(None, None, "row", "col"),
        P(None, None, "row"),
        P(None, None, ("row", "col")),
        P(None, None, ("row", "col")),
    )
    out_specs = (
        P(None, None, ("row", "col")),
        P(None, None, ("row", "col")),
        P(None, None, ("row", "col")),
    )
    return jax.shard_map(body, mesh=mesh, in_specs=in_specs, out_specs=out_specs, check_vma=False)
```

```python
import functools

import jax
import jax.numpy as jnp
from jax import lax
from jax.experimental import pallas as pl
from jax.experimental.pallas import tpu as pltpu
from jax.sharding import PartitionSpec as P

MESH = pl.DeviceIdType.MESH
GATES = 4
LOCAL_VMEM = 67_043_328


def lstm_cell(gate_total, cell_state):
    input_gate = jax.nn.sigmoid(gate_total[:, 0])
    forget_gate = jax.nn.sigmoid(gate_total[:, 1])
    candidate = jnp.tanh(gate_total[:, 2])
    output_gate = jax.nn.sigmoid(gate_total[:, 3])
    cell_state = forget_gate * cell_state + input_gate * candidate
    return (cell_state, (output_gate * jnp.tanh(cell_state)).astype(jnp.bfloat16))


def general_body(inputs, w_input, w_recur, gate_bias, hidden_init, cell_init):
    col_place = lax.axis_index("col")
    unit_width = hidden_init.shape[2]
    layers = w_input.shape[0]
    block_rows = w_input.shape[2]

    def project(vectors, weight):
        result = lax.dot_general(
            vectors,
            weight.reshape(-1, weight.shape[-1]),
            (((1,), (1,)), ((), ())),
            preferred_element_type=jnp.float32,
        )
        return result.reshape(vectors.shape[:-1] + (GATES, block_rows))

    def to_columns(owned):
        return lax.all_gather(owned, "row", axis=1, tiled=True)

    def gate_sums(partial_value, layer):
        bias_part = lax.dynamic_slice_in_dim(
            gate_bias[layer], col_place * unit_width, unit_width, 1
        )
        return (
            lax.psum_scatter(
                partial_value.astype(jnp.bfloat16), "col", scatter_dimension=2, tiled=True
            ).astype(jnp.float32)
            + bias_part[None]
        )

    start = tuple(
        (hidden_init[layer], to_columns(hidden_init[layer]), cell_init[layer])
        for layer in range(layers)
    )

    def advance_time(carried, step_item):
        lower, following = step_item, []
        for layer in range(layers):
            _, columns, cell_state = carried[layer]
            partial_value = project(lower, w_input[layer]) + project(columns, w_recur[layer])
            cell_state, owned = lstm_cell(gate_sums(partial_value, layer), cell_state)
            lower = to_columns(owned)
            following.append((owned, lower, cell_state))
        return tuple(following), following[-1][0]

    carried, top_hidden = lax.scan(advance_time, start, inputs)
    return (
        top_hidden,
        jnp.stack([item[0] for item in carried]),
        jnp.stack([item[2] for item in carried]),
    )


def xor(value, mask, size):
    total, bit = 0, 1
    while bit < size:
        total = total + bit * ((value // bit + mask // bit) % 2)
        bit *= 2
    return total


def window_kernel(
    n_row, n_col,
    inputs_in, w_input, w_recur, gate_bias_in, hidden_init_in, cell_init_in,
    hiddens, cells,
    inputs, gate_bias, hidden_init, cell_init,
    first, second, third, sums, sent, arrived, columns, small_sem,
    first_sem, first_again_sem, second_sem, third_sem,
    part_send, part_recv, block_send, block_recv,
):
    row, col = lax.axis_index("row"), lax.axis_index("col")
    unit = hidden_init.shape[2]
    batch = hidden_init.shape[1]
    chips = n_row // 2
    last = n_col - 1
    sibling = row + 1 - 2 * (row % 2)

    def owner_of(i):
        return xor(col, last - i, n_col)

    def load(weight, layer, buffer, sems, i, g):
        start = pl.multiple_of(owner_of(i) * unit, unit)
        k = i * GATES + g
        return pltpu.make_async_copy(
            weight.at[layer, g, pl.ds(start, unit), :], buffer.at[k], sems.at[k]
        )

    def far(k):
        return (row + 2 * k) % n_row

    def near(k):
        return (row + n_row - 2 * k) % n_row

    def send_block(which, source, owner, target, slot):
        return pltpu.make_async_remote_copy(
            src_ref=source,
            dst_ref=columns.at[which, owner],
            send_sem=block_send.at[which, slot],
            recv_sem=block_recv.at[which, slot],
            device_id=(target, col),
            device_id_type=MESH,
        )

    def gather_start(which, source):
        for k in range(1, chips):
            send_block(which, source, row, far(k), k).start()
        send_block(which, source, row, sibling, 0).start()

    def gather_forward(which):
        for k in range(1, chips):
            owner = near(k)
            send_block(which, columns.at[which, owner], owner, far(k), k).wait_recv()
            send_block(
                which, columns.at[which, owner], owner, sibling, chips - 1 + k
            ).start()

    def gather_wait(which):
        block = columns.at[which, sibling]
        send_block(which, block, sibling, sibling, 0).wait_recv()
        for k in range(1, chips):
            block = columns.at[which, (sibling + n_row - 2 * k) % n_row]
            send_block(which, block, row, sibling, chips - 1 + k).wait_recv()

    def gather_end(which):
        for slot in range(2 * chips - 1):
            send_block(which, columns.at[which, row], row, sibling, slot).wait_send()

    def vectors(which):
        return jnp.concatenate([columns[which, r] for r in range(n_row)], axis=1)

    def product(left, buffer, k):
        return lax.dot_general(
            buffer[k], left, (((1,), (1,)), ((), ())), preferred_element_type=jnp.float32
        ).T

    def send_part(which, i):
        return pltpu.make_async_remote_copy(
            src_ref=sent.at[which, i],
            dst_ref=arrived.at[which, i],
            send_sem=part_send.at[which, i],
            recv_sem=part_recv.at[which, i],
            device_id=(row, owner_of(i)),
            device_id_type=MESH,
        )

    def finish(which, held, buffer, i):
        left = vectors(held)
        totals = []
        for g in range(GATES):
            k = i * GATES + g
            totals.append(sums[which, k] + product(left, buffer, k))

        @pl.when(i < last)
        def _():
            for g in range(GATES):
                sent[which, i, g] = totals[g].astype(jnp.bfloat16)
            send_part(which, i).start()

        @pl.when(i == last)
        def _():
            for g in range(GATES):
                sums[which, last * GATES + g] = totals[g]

    def cell_step(which, layer, old_cell):
        for i in range(last):
            send_part(which, i).wait_recv()
        totals = []
        for g in range(GATES):
            total = sums[which, last * GATES + g]
            for i in range(last):
                total = total + arrived[which, i, g].astype(jnp.float32)
            bias = gate_bias[layer, pl.ds(g, 1), pl.ds(pl.multiple_of(col * unit, unit), unit)]
            totals.append(total + bias)
        cell = jax.nn.sigmoid(totals[1]) * old_cell + jax.nn.sigmoid(totals[0]) * jnp.tanh(totals[2])
        hidden = (jax.nn.sigmoid(totals[3]) * jnp.tanh(cell)).astype(jnp.bfloat16)
        return cell, hidden

    def loop(begin, end, step):
        def run(i, carried):
            step(i)
            return carried
        lax.fori_loop(begin, end, run, 0)

    small = [
        pltpu.make_async_copy(source, target, small_sem.at[k])
        for k, (source, target) in enumerate((
            (hidden_init_in, hidden_init),
            (inputs_in, inputs),
            (gate_bias_in, gate_bias),
            (cell_init_in, cell_init),
        ))
    ]
    for copy in small:
        copy.start()

    streams = (
        (w_input, 0, first, first_sem),
        (w_recur, 0, second, second_sem),
        (w_recur, 1, first, first_again_sem),
        (w_input, 1, third, third_sem),
    )
    ahead = min(2, n_col)

    def load_start(which, i):
        for g in range(GATES):
            load(*streams[which], i, g).start()

    def load_wait(which, i):
        for g in range(GATES):
            load(*streams[which], i, g).wait()

    def next_loads(which, i):
        @pl.when(i + ahead < n_col)
        def _():
            load_start(which, i + ahead)

        if which + 1 < len(streams):
            @pl.when(i + ahead >= n_col)
            def _():
                load_start(which + 1, i + ahead - n_col)

    for i in range(ahead):
        load_start(0, i)

    barrier = pltpu.get_barrier_semaphore()
    targets = [(sibling, col)]
    targets += [(far(k), col) for k in range(1, chips)]
    targets += [(row, owner_of(i)) for i in range(last)]
    for target in targets:
        pl.semaphore_signal(barrier, inc=1, device_id=target, device_id_type=MESH)
    pl.semaphore_wait(barrier, len(targets))

    small[0].wait()
    for layer in range(2):
        gather_start(layer, hidden_init.at[layer])
        columns[layer, row] = hidden_init[layer]

    for copy in small[1:]:
        copy.wait()

    def input_products(i):
        load_wait(0, i)
        next_loads(0, i)
        left = inputs[...].reshape(2 * batch, inputs.shape[2])
        for g in range(GATES):
            k = i * GATES + g
            both = product(left, first, k)
            sums[0, k] = both[:batch]
            sums[1, k] = both[batch:]

    half = n_col // 2
    loop(0, half, input_products)
    gather_forward(0)
    loop(half, n_col, input_products)
    gather_forward(1)
    gather_wait(0)

    def layer0_step0(i):
        load_wait(1, i)
        next_loads(1, i)
        finish(0, 0, second, i)

    loop(0, n_col, layer0_step0)
    gather_wait(1)

    def early_recurrent(i):
        load_wait(2, i)
        next_loads(2, i)
        left = vectors(1)
        for g in range(GATES):
            k = i * GATES + g
            sums[2, k] = product(left, first, k)

    loop(0, half, early_recurrent)
    cell, hidden = cell_step(0, 0, cell_init[0])
    columns[2, row] = hidden
    gather_start(2, columns.at[2, row])
    cells[0] = cell
    loop(half, n_col, early_recurrent)
    for i in range(ahead, n_col):
        load_start(3, i)
    gather_forward(2)
    gather_wait(2)

    loop(0, n_col, lambda i: finish(1, 2, second, i))

    def layer1_step0(i):
        load_wait(3, i)
        finish(2, 2, third, i)

    loop(0, half, layer1_step0)
    cell, hidden = cell_step(1, 0, cells[0])
    columns[3, row] = hidden
    gather_start(3, columns.at[3, row])
    cells[0] = cell
    hiddens[2] = hidden
    loop(half, n_col, layer1_step0)
    gather_forward(3)
    cell, hidden = cell_step(2, 1, cell_init[1])
    columns[4, row] = hidden
    gather_start(4, columns.at[4, row])
    cells[1] = cell
    hiddens[0] = hidden
    gather_wait(3)

    def late_input(i):
        left = vectors(3)
        for g in range(GATES):
            k = i * GATES + g
            sums[3, k] = product(left, third, k)

    loop(0, last, late_input)
    gather_forward(4)
    loop(last, n_col, late_input)
    gather_wait(4)
    loop(0, n_col, lambda i: finish(3, 4, first, i))
    cell, hidden = cell_step(3, 1, cells[1])
    cells[1] = cell
    hiddens[1] = hidden

    for which in range(5):
        gather_end(which)
    for which in range(4):
        for i in range(last):
            send_part(which, i).wait_send()


def output_kernel(hiddens, cells, top_hidden, final_hidden, final_cell):
    top_hidden[...] = hiddens[:2]
    final_hidden[0] = hiddens[2]
    final_hidden[1] = hiddens[1]
    final_cell[...] = cells[...]


def window_body(n_row, n_col, inputs, w_input, w_recur, gate_bias, hidden_init, cell_init):
    batch, unit = hidden_init.shape[1:]
    depth = w_input.shape[3]
    chunks = n_col * GATES
    chips = n_row // 2
    vmem = pl.BlockSpec(memory_space=pltpu.VMEM)
    hbm = pl.BlockSpec(memory_space=pl.ANY)
    hiddens, cells = pl.pallas_call(
        functools.partial(window_kernel, n_row, n_col),
        out_shape=(
            jax.ShapeDtypeStruct((3, batch, unit), jnp.bfloat16),
            jax.ShapeDtypeStruct((2, batch, unit), jnp.float32),
        ),
        in_specs=[hbm] * 6,
        out_specs=(vmem, vmem),
        scratch_shapes=[
            pltpu.VMEM(inputs.shape, inputs.dtype),
            pltpu.VMEM(gate_bias.shape, gate_bias.dtype),
            pltpu.VMEM(hidden_init.shape, hidden_init.dtype),
            pltpu.VMEM(cell_init.shape, cell_init.dtype),
            pltpu.VMEM((chunks, unit, depth), jnp.bfloat16),
            pltpu.VMEM((chunks, unit, depth), jnp.bfloat16),
            pltpu.VMEM((chunks, unit, depth), jnp.bfloat16),
            pltpu.VMEM((4, chunks, batch, unit), jnp.float32),
            pltpu.VMEM((4, n_col - 1, GATES, batch, unit), jnp.bfloat16),
            pltpu.VMEM((4, n_col - 1, GATES, batch, unit), jnp.bfloat16),
            pltpu.VMEM((5, n_row, batch, unit), jnp.bfloat16),
            pltpu.SemaphoreType.DMA((4,)),
            pltpu.SemaphoreType.DMA((chunks,)),
            pltpu.SemaphoreType.DMA((chunks,)),
            pltpu.SemaphoreType.DMA((chunks,)),
            pltpu.SemaphoreType.DMA((chunks,)),
            pltpu.SemaphoreType.DMA((4, n_col - 1)),
            pltpu.SemaphoreType.DMA((4, n_col - 1)),
            pltpu.SemaphoreType.DMA((5, 2 * chips - 1)),
            pltpu.SemaphoreType.DMA((5, 2 * chips - 1)),
        ],
        compiler_params=pltpu.CompilerParams(
            collective_id=0, has_side_effects=True, vmem_limit_bytes=LOCAL_VMEM
        ),
    )(inputs, w_input, w_recur, gate_bias, hidden_init, cell_init)
    return pl.pallas_call(
        output_kernel,
        out_shape=(
            jax.ShapeDtypeStruct((2, batch, unit), jnp.bfloat16),
            jax.ShapeDtypeStruct((2, batch, unit), jnp.bfloat16),
            jax.ShapeDtypeStruct((2, batch, unit), jnp.float32),
        ),
        in_specs=[vmem, vmem],
        out_specs=(vmem, vmem, vmem),
    )(hiddens, cells)


def solution(mesh):
    n_row, n_col = mesh.shape["row"], mesh.shape["col"]

    def body(inputs, w_input, w_recur, gate_bias, hidden_init, cell_init):
        unit = hidden_init.shape[2]
        held = 3 * w_input.size // w_input.shape[0] * 2
        fits = (
            inputs.shape[0] == 2
            and w_input.shape[0] == 2
            and unit % 128 == 0
            and n_row % 2 == 0
            and n_row >= 4
            and n_col >= 2
            and n_col & (n_col - 1) == 0
            and held + held // 4 < LOCAL_VMEM
        )
        args = (inputs, w_input, w_recur, gate_bias, hidden_init, cell_init)
        return window_body(n_row, n_col, *args) if fits else general_body(*args)

    in_specs = (
        P(None, None, "col"),
        P(None, None, "row", "col"),
        P(None, None, "row", "col"),
        P(None, None, "row"),
        P(None, None, ("row", "col")),
        P(None, None, ("row", "col")),
    )
    out_specs = (
        P(None, None, ("row", "col")),
        P(None, None, ("row", "col")),
        P(None, None, ("row", "col")),
    )
    return jax.shard_map(body, mesh=mesh, in_specs=in_specs, out_specs=out_specs, check_vma=False)
```
